32 devices in a mesh: seq: 16 (over z, x, core), head: 2 (over y).
Axes of the slice: x: 2, y: 2, z: 4, core: 2. Of those that a mesh axis runs over, the one named last changes fastest.
Arguments:
- fw_keys: bfloat16 [8192, 4096], P('seq', 'head'), may hold values from -6 to 6
- fw_values: bfloat16 [8192, 4096], P('seq', 'head'), may hold values from -6 to 6
- fw_queries: bfloat16 [8192, 4096], P('seq', 'head'), may hold values from -6 to 6
- rates: float32 [8192, 8], P('seq', 'head'), as said below
- w_gate: bfloat16 [8, 512, 512], P('head'), may hold values from -0.25 to 0.25
- w_up: bfloat16 [8, 512, 512], P('head'), may hold values from -0.25 to 0.25
- w_down: bfloat16 [8, 512, 512], P('head'), may hold values from -0.25 to 0.25
- out_gain: float32 [4096], P('head'), may hold values from 0.1 to 1.9
- att_query: bfloat16 [8192, 4096], P(('seq', 'head')), may hold values from -6 to 6
- att_key: bfloat16 [8192, 1024], P(('seq', 'head')), may hold values from -6 to 6
- att_value: bfloat16 [8192, 1024], P(('seq', 'head')), may hold values from -6 to 6
Outputs:
- block_out: bfloat16 [8192, 4096], P(('seq', 'head'))
The draws below stay inside these ranges and needn't reach their ends.
Inputs may be any that keep to these rules, and one draw needn't show every extreme that they name: Positive rates whose scale rises along the span by a factor of three, times per-token noise of 1 to 4.
All inputs are finite; a program needn't handle non-finite values.
Results may differ from the reference program's by a relative error of at most 0.0098.
Values may be sent and summed in bfloat16 or wider, within the bound.
A program may use at most 128 MiB of HBM per device.

```python
import jax
import jax.numpy as jnp
from jax import lax

FW_HEADS = 8
DH = 512
FW_HIDDEN = 512
QH = 32
KVH = 8
HD = 128
WINDOW = 256
D = 4096
TOKENS = 8192


def draw_rates(key, part):
    position = jnp.arange(TOKENS, dtype=jnp.float32) / TOKENS
    ramp = 1.0 + 2.0 * position
    noise = jnp.exp(jax.random.uniform(key, (TOKENS, FW_HEADS), jnp.float32, 0.0, jnp.log(4.0)))
    return 0.15 / jnp.sqrt(jnp.float32(TOKENS)) * ramp[:, None] * noise


def plant_events(key):
    events = TOKENS // WINDOW
    seeded = jax.random.fold_in(key, 91)
    sub_keys = jax.random.split(seeded, 6)
    half_window = max(WINDOW // 2, 1)
    quarter_window = max(WINDOW // 4, 1)
    first_pos = jnp.arange(events, dtype=jnp.int32) * WINDOW + jax.random.randint(sub_keys[0], (events,), 0, half_window, dtype=jnp.int32)
    second_pos = first_pos + jax.random.randint(sub_keys[1], (events,), 1, quarter_window + 1, dtype=jnp.int32)
    query_pos = second_pos + jax.random.randint(sub_keys[2], (events,), 0, quarter_window, dtype=jnp.int32)
    head_ids = jax.random.randint(sub_keys[3], (events,), 0, KVH, dtype=jnp.int32)
    direction = jnp.where(jax.random.bernoulli(sub_keys[4], 0.5, (events, HD)), 1.0, -1.0).astype(jnp.float32)
    strength = 3.5 + jax.random.randint(sub_keys[5], (events,), 0, 3, dtype=jnp.int32).astype(jnp.float32)
    return (first_pos, second_pos, query_pos, head_ids, direction, strength)


def base_field(key, dims):
    return jnp.clip(1.6 * jax.random.normal(key, dims, jnp.float32), -6.0, 6.0)


def draw_att_key(key, part):
    first_pos, second_pos, query_pos, head_ids, direction, strength = plant_events(key)
    baseline = base_field(jax.random.fold_in(key, 13), (TOKENS, KVH, HD))
    key_level = 4.5
    baseline = baseline.at[first_pos, head_ids].set(key_level * direction)
    baseline = baseline.at[second_pos, head_ids].set((key_level - 0.03125) * direction)
    return baseline.reshape(TOKENS, KVH * HD).astype(jnp.bfloat16)


def draw_att_query(key, part):
    first_pos, second_pos, query_pos, head_ids, direction, strength = plant_events(key)
    group = QH // KVH
    baseline = base_field(jax.random.fold_in(key, 29), (TOKENS, KVH, group, HD))
    planted = strength[:, None, None] * direction[:, None, :]
    baseline = baseline.at[query_pos, head_ids].set(jnp.broadcast_to(planted, (TOKENS // WINDOW, group, HD)))
    return baseline.reshape(TOKENS, QH * HD).astype(jnp.bfloat16)


def block_scale(rng, shape, cuts, least, high):
    factor_of, own = 1.0, jax.random.fold_in(rng, 6)
    for dim, blocks in cuts:
        draws = jnp.exp(jax.random.uniform(jax.random.fold_in(own, dim), (blocks,), jnp.float32, least / len(cuts), high / len(cuts)))
        factor_of = factor_of * jnp.repeat(draws, shape[dim] // blocks).reshape([-1 if axis == dim else 1 for axis in range(len(shape))])
    return factor_of


def bell_draw(stream_key, shape, scale, bound, pieces=(), held_as=jnp.bfloat16):
    result = jax.random.normal(stream_key, shape, jnp.float32) * scale
    if len(pieces) > 0:
        result = block_scale(stream_key, shape, pieces, -0.22, 0.18) * result
    return jnp.clip(result, min=-bound, max=bound).astype(held_as)


def setup_inputs(seed: int = 0) -> dict:
    streams_of = jax.random.split(jax.random.key(seed), 12)
    fw_keys = bell_draw(streams_of[0], (TOKENS, D), 1.0, 6.0, ((0, 16), (1, 2)))
    fw_values = bell_draw(streams_of[1], (TOKENS, D), 1.0, 6.0, ((0, 16), (1, 2)))
    fw_queries = bell_draw(streams_of[2], (TOKENS, D), 1.0, 6.0, ((0, 16), (1, 2)))
    rates = draw_rates(jax.random.fold_in(streams_of[11], 71), 0)
    w_gate = bell_draw(streams_of[4], (FW_HEADS, FW_HIDDEN, DH), DH ** -0.5, 0.25, ((0, 2),))
    w_up = bell_draw(streams_of[5], (FW_HEADS, FW_HIDDEN, DH), DH ** -0.5, 0.25, ((0, 2),))
    w_down = bell_draw(streams_of[6], (FW_HEADS, FW_HIDDEN, DH), FW_HIDDEN ** -0.5, 0.25, ((0, 2),))
    out_gain = jnp.clip(1.0 + 0.18 * jax.random.normal(streams_of[7], (D,), jnp.float32), 0.1, 1.9)
    att_query = draw_att_query(jax.random.fold_in(streams_of[11], 71), 0)
    att_key = draw_att_key(jax.random.fold_in(streams_of[11], 71), 0)
    att_value = bell_draw(streams_of[10], (TOKENS, KVH * HD), 1.0, 6.0, ((0, 32),))
    return {"fw_keys": fw_keys, "fw_values": fw_values, "fw_queries": fw_queries, "rates": rates, "w_gate": w_gate, "w_up": w_up, "w_down": w_down, "out_gain": out_gain, "att_query": att_query, "att_key": att_key, "att_value": att_value}


def fast_hidden(x, w_gate, w_up):
    gate = jnp.dot(x, w_gate.T, preferred_element_type=jnp.float32)
    up = jnp.dot(x, w_up.T, preferred_element_type=jnp.float32)
    return (gate, up, (jax.nn.silu(gate) * up).astype(jnp.bfloat16))

def head_grads(keys, values, rate_col, w_gate, w_up, w_down):
    gate, up, hidden = fast_hidden(keys, w_gate, w_up)
    dval = (-rate_col[:, None] * values.astype(jnp.float32)).astype(jnp.bfloat16)
    g_down = jnp.dot(hidden.T, dval, preferred_element_type=jnp.float32)
    dhid = jnp.dot(dval, w_down.T, preferred_element_type=jnp.float32)
    sig = jax.nn.sigmoid(gate)
    d_gate = (dhid * up * sig * (1.0 + gate * (1.0 - sig))).astype(jnp.bfloat16)
    d_up = (dhid * (gate * sig)).astype(jnp.bfloat16)
    g_gate = jnp.dot(d_gate.T, keys, preferred_element_type=jnp.float32)
    g_up = jnp.dot(d_up.T, keys, preferred_element_type=jnp.float32)
    return jnp.stack([g_gate, g_up, g_down])

def renorm(old, grads):
    old = old.astype(jnp.float32)
    fresh = old - grads
    scale = jnp.sqrt(lax.optimization_barrier(jnp.sum(old * old, axis=-1, keepdims=True))) / jnp.sqrt(lax.optimization_barrier(jnp.sum(fresh * fresh, axis=-1, keepdims=True)) + 1e-06)
    return (fresh * scale).astype(jnp.bfloat16)

def apply_head(queries, weights, gain):
    gate, up, hidden = fast_hidden(queries, weights[0], weights[1])
    raw = jnp.dot(hidden, weights[2], preferred_element_type=jnp.float32)
    normed = raw * lax.rsqrt(lax.optimization_barrier(jnp.mean(raw * raw, axis=-1, keepdims=True)) + 1e-06) * gain
    return normed.astype(jnp.bfloat16)

def reference(fw_keys, fw_values, fw_queries, rates, w_gate, w_up, w_down, out_gain, att_query, att_key, att_value):

    def split(arr):
        return arr.reshape(TOKENS, FW_HEADS, DH).transpose(1, 0, 2)

    def one_head(packed):
        keys, values, queries, rate_col, wg, wu, wd, gain = packed
        grads = head_grads(keys, values, rate_col, wg, wu, wd)
        weights = renorm(jnp.stack([wg, wu, wd]), grads)
        return apply_head(queries, weights, gain)
    fw_heads = lax.map(one_head, (split(fw_keys), split(fw_values), split(fw_queries), rates.T, w_gate, w_up, w_down, out_gain.reshape(FW_HEADS, DH)))
    fw_out = fw_heads.transpose(1, 0, 2).reshape(TOKENS, D)
    group = QH // KVH
    query = att_query.reshape(TOKENS, KVH, group, HD)
    pad = jnp.zeros((WINDOW, KVH, HD), jnp.bfloat16)
    key_pad = jnp.concatenate([pad, att_key.reshape(TOKENS, KVH, HD)], axis=0)
    val_pad = jnp.concatenate([pad, att_value.reshape(TOKENS, KVH, HD)], axis=0)

    def block(index):
        start = (index * WINDOW).astype(jnp.int32)
        qblk = lax.dynamic_slice_in_dim(query, start, WINDOW, 0).astype(jnp.float32)
        kblk = lax.dynamic_slice_in_dim(key_pad, start, 2 * WINDOW, 0).astype(jnp.float32)
        vblk = lax.dynamic_slice_in_dim(val_pad, start, 2 * WINDOW, 0).astype(jnp.float32)
        scores = jnp.einsum('rkgd,skd->kgrs', qblk, kblk) / jnp.sqrt(jnp.float32(HD))
        qpos = start + jnp.arange(WINDOW, dtype=jnp.int32)
        kpos = start - WINDOW + jnp.arange(2 * WINDOW, dtype=jnp.int32)
        valid = (kpos[None, :] >= 0) & (kpos[None, :] <= qpos[:, None]) & (kpos[None, :] > qpos[:, None] - WINDOW)
        scores = jnp.where(valid, scores, -1e+30)
        peak = lax.optimization_barrier(jnp.max(scores, axis=-1, keepdims=True))
        expo = jnp.exp(scores - peak)
        probs = (expo / lax.optimization_barrier(jnp.sum(expo, axis=-1, keepdims=True))).astype(jnp.bfloat16)
        out = jnp.einsum('kgrs,skd->rkgd', probs.astype(jnp.float32), vblk)
        return out.reshape(WINDOW, D)
    attn = lax.map(block, jnp.arange(TOKENS // WINDOW, dtype=jnp.int32)).reshape(TOKENS, D)
    return (attn + fw_out.astype(jnp.float32)).astype(jnp.bfloat16)
```

```python
import functools

import jax
import jax.numpy as jnp
from jax import lax
from jax.experimental import pallas as pl
from jax.experimental.pallas import tpu as pltpu
from jax.sharding import PartitionSpec as P

HD = 128
WINDOW = 256


def from_behind(block, axis, distance):
    devices = range(lax.axis_size(axis))
    route = [(i - distance, i) for i in devices if i - distance in devices]
    return lax.ppermute(block, axis, route)


def fast_hidden(inputs, w_gate, w_up):
    gate = jnp.dot(inputs, w_gate.T, preferred_element_type=jnp.float32)
    up = jnp.dot(inputs, w_up.T, preferred_element_type=jnp.float32)
    return (gate, up, (jax.nn.silu(gate) * up).astype(jnp.bfloat16))


def head_grads(keys, values, rate_col, w_gate, w_up, w_down):
    gate, up, hidden = fast_hidden(keys, w_gate, w_up)
    dval = (-rate_col[:, None] * values.astype(jnp.float32)).astype(jnp.bfloat16)
    g_down = jnp.dot(hidden.T, dval, preferred_element_type=jnp.float32)
    dhid = jnp.dot(dval, w_down.T, preferred_element_type=jnp.float32)
    sig = jax.nn.sigmoid(gate)
    d_gate = (dhid * up * sig * (1.0 + gate * (1.0 - sig))).astype(jnp.bfloat16)
    d_up = (dhid * (gate * sig)).astype(jnp.bfloat16)
    g_gate = jnp.dot(d_gate.T, keys, preferred_element_type=jnp.float32)
    g_up = jnp.dot(d_up.T, keys, preferred_element_type=jnp.float32)
    return jnp.stack([g_gate, g_up, g_down])


def renorm(old, grads):
    old = old.astype(jnp.float32)
    fresh = old - grads
    scale = jnp.sqrt(jnp.sum(old * old, axis=-1, keepdims=True)) / jnp.sqrt(
        jnp.sum(fresh * fresh, axis=-1, keepdims=True) + 1e-06
    )
    return (fresh * scale).astype(jnp.bfloat16)


def apply_head(queries, weights, gain):
    gate, up, hidden = fast_hidden(queries, weights[0], weights[1])
    raw = jnp.dot(hidden, weights[2], preferred_element_type=jnp.float32)
    normed = raw * lax.rsqrt(jnp.mean(raw * raw, axis=-1, keepdims=True) + 1e-06) * gain
    return normed.astype(jnp.bfloat16)


def plain_device(
    fw_keys,
    fw_values,
    fw_queries,
    rates,
    w_gate,
    w_up,
    w_down,
    out_gain,
    att_query,
    att_key,
    att_value,
):
    local_heads = w_gate.shape[0]
    width = w_gate.shape[2]
    stacked = jnp.stack([w_gate, w_up, w_down], axis=1)
    grad_list = []
    for head in range(local_heads):
        cols = slice(head * width, (head + 1) * width)
        grad_list.append(
            head_grads(
                fw_keys[:, cols],
                fw_values[:, cols],
                rates[:, head],
                w_gate[head],
                w_up[head],
                w_down[head],
            )
        )
    local_grads = jnp.stack(grad_list)
    shares = lax.psum_scatter(local_grads, "seq", scatter_dimension=2, tiled=True)
    count = shares.shape[2]
    first = lax.axis_index("seq") * count
    old_rows = lax.dynamic_slice_in_dim(stacked, first, count, 2)
    weights = lax.all_gather(renorm(old_rows, shares), "seq", axis=2, tiled=True)
    out_list = []
    for head in range(local_heads):
        cols = slice(head * width, (head + 1) * width)
        out_list.append(apply_head(fw_queries[:, cols], weights[head], out_gain[cols]))
    fw_local = jnp.concatenate(out_list, axis=1)
    fw_tok = lax.all_to_all(fw_local, "head", split_axis=0, concat_axis=1, tiled=True)
    rows = att_query.shape[0]
    kv_heads = att_key.shape[1] // HD
    group = att_query.shape[1] // HD // kv_heads
    reach = (WINDOW - 1) // rows + 1
    pair = jnp.stack([att_key, att_value])
    earlier = []
    moving = pair
    for step in range(reach):
        moving = from_behind(moving, ("seq", "head"), 1)
        earlier.insert(0, moving)
    window_kv = jnp.concatenate(earlier + [pair], axis=1)
    keys = window_kv[0].reshape(-1, kv_heads, HD)
    values = window_kv[1].reshape(-1, kv_heads, HD)
    base = (lax.axis_index("seq") * lax.axis_size("head") + lax.axis_index("head")) * rows
    qpos = base + jnp.arange(rows, dtype=jnp.int32)
    kpos = base - reach * rows + jnp.arange((reach + 1) * rows, dtype=jnp.int32)
    valid = (
        (kpos[None, :] >= 0)
        & (kpos[None, :] <= qpos[:, None])
        & (kpos[None, :] > qpos[:, None] - WINDOW)
    )
    query = att_query.reshape(rows, kv_heads, group, HD)
    scores = jnp.einsum(
        "rkgd,skd->kgrs", query, keys, preferred_element_type=jnp.float32
    ) / jnp.sqrt(jnp.float32(HD))
    scores = jnp.where(valid, scores, -1e30)
    peak = jnp.max(scores, axis=-1, keepdims=True)
    expo = jnp.exp(scores - peak)
    probs = (expo / jnp.sum(expo, axis=-1, keepdims=True)).astype(jnp.bfloat16)
    attn = jnp.einsum("kgrs,skd->rkgd", probs, values, preferred_element_type=jnp.float32).reshape(
        rows, -1
    )
    return (attn + fw_tok.astype(jnp.float32)).astype(jnp.bfloat16)


F32 = jnp.float32
BF16 = jnp.bfloat16
MESH = pl.DeviceIdType.MESH
NT = (((1,), (1,)), ((), ()))
TN = (((0,), (0,)), ((), ()))
NN = (((1,), (0,)), ((), ()))


def mm(a, b, dims):
    return lax.dot_general(a, b, dims, preferred_element_type=F32)


def grads_kernel(k_ref, v_ref, rate_ref, wg_ref, wu_ref, wd_ref, out_ref):
    head = pl.program_id(0)
    keys = k_ref[...]
    lane = lax.broadcasted_iota(jnp.int32, rate_ref.shape, 1)
    rate = jnp.sum(jnp.where(lane == head, rate_ref[...], 0.0), axis=1, keepdims=True)
    gate = mm(keys, wg_ref[0], NT)
    up = mm(keys, wu_ref[0], NT)
    sig = jax.nn.sigmoid(gate)
    silu = gate * sig
    hidden = (silu * up).astype(BF16)
    dval = (-rate * v_ref[...].astype(F32)).astype(BF16)
    out_ref[2] = mm(hidden, dval, TN).astype(BF16)
    dhid = mm(dval, wd_ref[0], NT)
    d_gate = (dhid * up * sig * (1.0 + gate * (1.0 - sig))).astype(BF16)
    out_ref[0] = mm(d_gate, keys, TN).astype(BF16)
    d_up = (dhid * silu).astype(BF16)
    out_ref[1] = mm(d_up, keys, TN).astype(BF16)


def local_grads_call(keys, values, rates, w_gate, w_up, w_down):
    heads, hidden, width = w_gate.shape
    tokens = keys.shape[0]
    col = pl.BlockSpec((tokens, width), lambda h: (0, h))
    mat = pl.BlockSpec((1, hidden, width), lambda h: (h, 0, 0))
    flops = heads * 12 * tokens * hidden * width
    return pl.pallas_call(
        grads_kernel,
        grid=(heads,),
        in_specs=[col, col, pl.BlockSpec(rates.shape, lambda h: (0, 0)), mat, mat, mat],
        out_specs=pl.BlockSpec((3, hidden, width), lambda h: (h, 0, 0)),
        out_shape=jax.ShapeDtypeStruct((heads * 3, hidden, width), BF16),
        cost_estimate=pl.CostEstimate(
            flops=flops, bytes_accessed=20 * 2**20, transcendentals=heads * tokens * hidden
        ),
        compiler_params=pltpu.CompilerParams(vmem_limit_bytes=40 * 2**20),
    )(keys, values, rates, w_gate, w_up, w_down)


def block_kernel(
    levels,
    g_ref,
    old_ref,
    fwq_ref,
    gain_ref,
    q_ref,
    kp_ref,
    vp_ref,
    k_ref,
    v_ref,
    out_ref,
    fresh,
    total,
    core_in,
    *rest,
):
    seq = lax.axis_index("seq")
    side = lax.axis_index("head")
    steps = len(levels)
    row_in = rest[:steps]
    (attn, bias, fw_out, fw_in, core_sems, rs_sems, ag_sems, out_sems, fw_sems) = rest[steps:]
    mats, hidden, width = total.shape
    rows = q_ref.shape[0]
    local_heads = fwq_ref.shape[1] // width
    kv_heads = k_ref.shape[1] // HD
    group = q_ref.shape[1] // HD // kv_heads
    core = lax.rem(seq, 2)

    def partner(bit):
        return seq + bit * (1 - 2 * lax.rem(seq // bit, 2))

    barrier = pltpu.get_barrier_semaphore()
    for bit in (1,) + levels:
        pl.semaphore_signal(
            barrier, inc=1, device_id=(partner(bit), side), device_id_type=MESH
        )
    pl.semaphore_signal(barrier, inc=1, device_id=(seq, 1 - side), device_id_type=MESH)
    pl.semaphore_wait(barrier, steps + 2)

    pending = []

    def send(src, dst, sems, where, target):
        copy = pltpu.make_async_remote_copy(
            src_ref=src,
            dst_ref=dst,
            send_sem=sems.at[(0,) + where],
            recv_sem=sems.at[(1,) + where],
            device_id=target,
            device_id_type=MESH,
        )
        copy.start()
        pending.append(copy)
        return copy

    offsets = [0]
    for i, bit in enumerate(levels):
        offsets.append(offsets[-1] + lax.rem(seq // bit, 2) * (hidden >> (i + 1)))

    def held(i):
        size = hidden >> i
        return pl.ds(pl.multiple_of(offsets[i], size) if i else 0, size)

    def given(i):
        size = hidden >> (i + 1)
        bit = lax.rem(seq // levels[i], 2)
        return pl.ds(pl.multiple_of(offsets[i] + (1 - bit) * size, size), size)

    first = core * mats
    other = (1 - core) * mats
    core_copies = [
        send(g_ref.at[other + m], core_in.at[m], core_sems, (m,), (partner(1), side))
        for m in range(mats)
    ]
    rs = {}
    ag = {}

    def reduce_send(i, m):
        rs[i, m] = send(
            total.at[m, given(i)],
            row_in[i].at[m],
            rs_sems,
            (i, m),
            (partner(levels[i]), side),
        )

    def core_sum(m):
        core_copies[m].wait_recv()
        total[m] = (g_ref[first + m].astype(F32) + core_in[m].astype(F32)).astype(BF16)
        reduce_send(0, m)

    def gather_send(i, m):
        where = fresh.at[first + m, held(i + 1)]
        ag[i, m] = send(where, where, ag_sems, (i, m), (partner(levels[i]), side))

    def row_sum(i, m):
        rs[i, m].wait_recv()
        part = total[m, held(i + 1)].astype(F32) + row_in[i][m].astype(F32)
        if i + 1 < steps:
            total[m, held(i + 1)] = part.astype(BF16)
            reduce_send(i + 1, m)
        else:
            old = old_ref[m].astype(F32)
            new = old - part
            scale = jnp.sqrt(jnp.sum(old * old, axis=-1, keepdims=True)) / jnp.sqrt(
                jnp.sum(new * new, axis=-1, keepdims=True) + 1e-06
            )
            fresh[first + m, held(steps)] = (new * scale).astype(BF16)
            gather_send(steps - 1, m)

    def gathered(i, m):
        ag[i, m].wait_recv()
        if i > 0:
            gather_send(i - 1, m)
        else:
            where = fresh.at[first + m]
            ag[-1, m] = send(where, where, out_sems, (m,), (partner(1), side))

    def attend(kv):
        cols = slice(kv * HD, (kv + 1) * HD)
        keys = jnp.concatenate([kp_ref[:, cols], k_ref[:, cols]], axis=0)
        values = jnp.concatenate([vp_ref[:, cols], v_ref[:, cols]], axis=0)

        def one(j, carry):
            at = pl.ds(pl.multiple_of((kv * group + j) * HD, HD), HD)
            scores = mm(q_ref[:, at], keys, NT) * (HD**-0.5) + bias[...]
            expo = jnp.exp(scores - jnp.max(scores, axis=-1, keepdims=True))
            probs = (expo / jnp.sum(expo, axis=-1, keepdims=True)).astype(BF16)
            attn[:, at] = mm(probs, values, NN)
            return carry

        lax.fori_loop(0, group, one, 0)

    def apply_rows(head, start):
        cols = pl.ds(pl.multiple_of(head * width, width), width)
        query = fwq_ref[pl.ds(pl.multiple_of(start, rows), rows), cols]
        gate = mm(query, fresh[head * 3], NT)
        up = mm(query, fresh[head * 3 + 1], NT)
        mid = (gate * jax.nn.sigmoid(gate) * up).astype(BF16)
        raw = mm(mid, fresh[head * 3 + 2], NN)
        mean = jnp.mean(raw * raw, axis=-1, keepdims=True)
        return (raw * lax.rsqrt(mean + 1e-06) * gain_ref[:, cols]).astype(BF16)

    fw = {}

    def apply(slot, head):
        fw_out[slot] = apply_rows(head, (1 - side) * rows)
        fw[slot] = send(fw_out.at[slot], fw_in.at[slot], fw_sems, (slot,), (seq, 1 - side))
        mine = apply_rows(head, side * rows)
        at = pl.ds(pl.multiple_of((side * local_heads + head) * width, width), width)
        out_ref[:, at] = (attn[:, at] + mine.astype(F32)).astype(BF16)

    def finish(slot, head):
        fw[slot].wait_recv()
        at = pl.ds(pl.multiple_of(((1 - side) * local_heads + head) * width, width), width)
        out_ref[:, at] = (attn[:, at] + fw_in[slot].astype(F32)).astype(BF16)

    base = (seq * 2 + side) * rows
    qpos = base + lax.broadcasted_iota(jnp.int32, bias.shape, 0)
    kpos = base - rows + lax.broadcasted_iota(jnp.int32, bias.shape, 1)
    valid = (kpos >= 0) & (kpos <= qpos) & (kpos > qpos - WINDOW)
    bias[...] = jnp.where(valid, 0.0, -1e30)

    for m in range(mats):
        core_sum(m)
    fillers = list(range(kv_heads))
    depth = 2 * steps
    for wave in range(mats + depth - 1):
        for i in range(steps):
            if 0 <= wave - i < mats:
                row_sum(i, wave - i)
        for j in range(steps - 1):
            if 0 <= wave - steps - j < mats:
                gathered(steps - 1 - j, wave - steps - j)
        take = 2 if len(fillers) > mats - 1 - wave else 1
        for _ in range(take):
            if fillers:
                attend(fillers.pop(0))
    for kv in fillers:
        attend(kv)
    half = local_heads // 2
    mine, theirs = core * half, (1 - core) * half
    for lh in range(half):
        for m in range(3 * lh, 3 * lh + 3):
            gathered(0, m)
        apply(lh, mine + lh)
        if lh > 0:
            for m in range(3 * lh - 3, 3 * lh):
                ag[-1, m].wait_recv()
            apply(half + lh - 1, theirs + lh - 1)
    for m in range(3 * half - 3, 3 * half):
        ag[-1, m].wait_recv()
    apply(2 * half - 1, theirs + half - 1)
    for lh in range(half):
        finish(lh, mine + lh)
        if lh > 0:
            finish(half + lh - 1, theirs + lh - 1)
    finish(2 * half - 1, theirs + half - 1)
    for copy in pending:
        copy.wait_send()


def per_device(
    fw_keys,
    fw_values,
    fw_queries,
    rates,
    w_gate,
    w_up,
    w_down,
    out_gain,
    att_query,
    att_key,
    att_value,
):
    count = lax.axis_size("seq")
    local_heads, hidden, width = w_gate.shape
    rows = att_query.shape[0]
    fits = (
        lax.axis_size("head") == 2
        and count >= 4
        and count & (count - 1) == 0
        and local_heads % 2 == 0
        and hidden * 2 // count >= 16
        and rows == WINDOW
    )
    if not fits:
        return plain_device(
            fw_keys,
            fw_values,
            fw_queries,
            rates,
            w_gate,
            w_up,
            w_down,
            out_gain,
            att_query,
            att_key,
            att_value,
        )
    before_k = from_behind(att_key, ("seq", "head"), 1)
    before_v = from_behind(att_value, ("seq", "head"), 1)
    grads = local_grads_call(fw_keys, fw_values, rates, w_gate, w_up, w_down)
    levels = []
    bit = 2
    while bit < count:
        levels.append(bit)
        bit *= 2
    levels = tuple(levels)
    steps = len(levels)
    seq = lax.axis_index("seq")
    offset = 0
    for i, bit in enumerate(levels):
        offset = offset + lax.rem(seq // bit, 2) * (hidden >> (i + 1))
    own = hidden >> steps
    half = local_heads // 2
    mats = 3 * half
    old = jnp.stack(
        [
            lax.dynamic_slice(w, (lax.rem(seq, 2) * half, offset, 0), (half, own, width))
            for w in (w_gate, w_up, w_down)
        ],
        axis=1,
    ).reshape(mats, own, width)
    dma = pltpu.SemaphoreType.DMA
    vmem = pl.BlockSpec(memory_space=pltpu.VMEM)
    return pl.pallas_call(
        functools.partial(block_kernel, levels),
        out_shape=jax.ShapeDtypeStruct(att_query.shape, BF16),
        in_specs=[vmem] * 9,
        out_specs=vmem,
        scratch_shapes=[
            pltpu.VMEM((2 * mats, hidden, width), BF16),
            pltpu.VMEM((mats, hidden, width), BF16),
            pltpu.VMEM((mats, hidden, width), BF16),
            *[pltpu.VMEM((mats, hidden >> (i + 1), width), BF16) for i in range(steps)],
            pltpu.VMEM(att_query.shape, F32),
            pltpu.VMEM((rows, 2 * rows), F32),
            pltpu.VMEM((local_heads, rows, width), BF16),
            pltpu.VMEM((local_heads, rows, width), BF16),
            dma((2, mats)),
            dma((2, steps, mats)),
            dma((2, steps, mats)),
            dma((2, mats)),
            dma((2, local_heads)),
        ],
        compiler_params=pltpu.CompilerParams(
            collective_id=0, has_side_effects=True, vmem_limit_bytes=60 * 2**20
        ),
    )(
        grads,
        old,
        fw_queries,
        out_gain.reshape(1, -1),
        att_query,
        before_k,
        before_v,
        att_key,
        att_value,
    )


def solution(mesh):
    return jax.shard_map(
        per_device,
        mesh=mesh,
        in_specs=(
            P("seq", "head"),
            P("seq", "head"),
            P("seq", "head"),
            P("seq", "head"),
            P("head", None, None),
            P("head", None, None),
            P("head", None, None),
            P("head"),
            P(("seq", "head"), None),
            P(("seq", "head"), None),
            P(("seq", "head"), None),
        ),
        out_specs=P(("seq", "head"), None),
        check_vma=False,
    )
```

```python
import functools

import jax
import jax.numpy as jnp
from jax import lax
from jax.experimental import pallas as pl
from jax.experimental.pallas import tpu as pltpu
from jax.sharding import PartitionSpec as P

HD = 128
WINDOW = 256


def from_behind(block, axis, distance):
    devices = range(lax.axis_size(axis))
    route = [(i - distance, i) for i in devices if i - distance in devices]
    return lax.ppermute(block, axis, route)


def fast_hidden(inputs, w_gate, w_up):
    gate = jnp.dot(inputs, w_gate.T, preferred_element_type=jnp.float32)
    up = jnp.dot(inputs, w_up.T, preferred_element_type=jnp.float32)
    return (gate, up, (jax.nn.silu(gate) * up).astype(jnp.bfloat16))


def head_grads(keys, values, rate_col, w_gate, w_up, w_down):
    gate, up, hidden = fast_hidden(keys, w_gate, w_up)
    dval = (-rate_col[:, None] * values.astype(jnp.float32)).astype(jnp.bfloat16)
    g_down = jnp.dot(hidden.T, dval, preferred_element_type=jnp.float32)
    dhid = jnp.dot(dval, w_down.T, preferred_element_type=jnp.float32)
    sig = jax.nn.sigmoid(gate)
    d_gate = (dhid * up * sig * (1.0 + gate * (1.0 - sig))).astype(jnp.bfloat16)
    d_up = (dhid * (gate * sig)).astype(jnp.bfloat16)
    g_gate = jnp.dot(d_gate.T, keys, preferred_element_type=jnp.float32)
    g_up = jnp.dot(d_up.T, keys, preferred_element_type=jnp.float32)
    return jnp.stack([g_gate, g_up, g_down])


def renorm(old, grads):
    old = old.astype(jnp.float32)
    fresh = old - grads
    scale = jnp.sqrt(jnp.sum(old * old, axis=-1, keepdims=True)) / jnp.sqrt(
        jnp.sum(fresh * fresh, axis=-1, keepdims=True) + 1e-06
    )
    return (fresh * scale).astype(jnp.bfloat16)


def apply_head(queries, weights, gain):
    gate, up, hidden = fast_hidden(queries, weights[0], weights[1])
    raw = jnp.dot(hidden, weights[2], preferred_element_type=jnp.float32)
    normed = raw * lax.rsqrt(jnp.mean(raw * raw, axis=-1, keepdims=True) + 1e-06) * gain
    return normed.astype(jnp.bfloat16)


def plain_device(
    fw_keys,
    fw_values,
    fw_queries,
    rates,
    w_gate,
    w_up,
    w_down,
    out_gain,
    att_query,
    att_key,
    att_value,
):
    local_heads = w_gate.shape[0]
    width = w_gate.shape[2]
    stacked = jnp.stack([w_gate, w_up, w_down], axis=1)
    grad_list = []
    for head in range(local_heads):
        cols = slice(head * width, (head + 1) * width)
        grad_list.append(
            head_grads(
                fw_keys[:, cols],
                fw_values[:, cols],
                rates[:, head],
                w_gate[head],
                w_up[head],
                w_down[head],
            )
        )
    local_grads = jnp.stack(grad_list)
    shares = lax.psum_scatter(local_grads, "seq", scatter_dimension=2, tiled=True)
    count = shares.shape[2]
    first = lax.axis_index("seq") * count
    old_rows = lax.dynamic_slice_in_dim(stacked, first, count, 2)
    weights = lax.all_gather(renorm(old_rows, shares), "seq", axis=2, tiled=True)
    out_list = []
    for head in range(local_heads):
        cols = slice(head * width, (head + 1) * width)
        out_list.append(apply_head(fw_queries[:, cols], weights[head], out_gain[cols]))
    fw_local = jnp.concatenate(out_list, axis=1)
    fw_tok = lax.all_to_all(fw_local, "head", split_axis=0, concat_axis=1, tiled=True)
    rows = att_query.shape[0]
    kv_heads = att_key.shape[1] // HD
    group = att_query.shape[1] // HD // kv_heads
    reach = (WINDOW - 1) // rows + 1
    pair = jnp.stack([att_key, att_value])
    earlier = []
    moving = pair
    for step in range(reach):
        moving = from_behind(moving, ("seq", "head"), 1)
        earlier.insert(0, moving)
    window_kv = jnp.concatenate(earlier + [pair], axis=1)
    keys = window_kv[0].reshape(-1, kv_heads, HD)
    values = window_kv[1].reshape(-1, kv_heads, HD)
    base = (lax.axis_index("seq") * lax.axis_size("head") + lax.axis_index("head")) * rows
    qpos = base + jnp.arange(rows, dtype=jnp.int32)
    kpos = base - reach * rows + jnp.arange((reach + 1) * rows, dtype=jnp.int32)
    valid = (
        (kpos[None, :] >= 0)
        & (kpos[None, :] <= qpos[:, None])
        & (kpos[None, :] > qpos[:, None] - WINDOW)
    )
    query = att_query.reshape(rows, kv_heads, group, HD)
    scores = jnp.einsum(
        "rkgd,skd->kgrs", query, keys, preferred_element_type=jnp.float32
    ) / jnp.sqrt(jnp.float32(HD))
    scores = jnp.where(valid, scores, -1e30)
    peak = jnp.max(scores, axis=-1, keepdims=True)
    expo = jnp.exp(scores - peak)
    probs = (expo / jnp.sum(expo, axis=-1, keepdims=True)).astype(jnp.bfloat16)
    attn = jnp.einsum("kgrs,skd->rkgd", probs, values, preferred_element_type=jnp.float32).reshape(
        rows, -1
    )
    return (attn + fw_tok.astype(jnp.float32)).astype(jnp.bfloat16)


F32 = jnp.float32
BF16 = jnp.bfloat16
MESH = pl.DeviceIdType.MESH
NT = (((1,), (1,)), ((), ()))
TN = (((0,), (0,)), ((), ()))
NN = (((1,), (0,)), ((), ()))


def mm(a, b, dims):
    return lax.dot_general(a, b, dims, preferred_element_type=F32)


def head_grads_tile(keys, values, rate, w_gate, w_up, w_down):
    gate = mm(keys, w_gate, NT)
    up = mm(keys, w_up, NT)
    sig = jax.nn.sigmoid(gate)
    silu = gate * sig
    hidden = (silu * up).astype(BF16)
    dval = (-rate * values.astype(F32)).astype(BF16)
    dhid = mm(dval, w_down, NT)
    yield 2, mm(hidden, dval, TN)
    d_gate = (dhid * up * sig * (1.0 + gate * (1.0 - sig))).astype(BF16)
    yield 0, mm(d_gate, keys, TN)
    d_up = (dhid * silu).astype(BF16)
    yield 1, mm(d_up, keys, TN)


def block_kernel(
    levels,
    fk_hbm,
    fv_hbm,
    fwq_hbm,
    wg_hbm,
    wu_hbm,
    wd_hbm,
    q_hbm,
    k_hbm,
    v_hbm,
    rate_ref,
    gain_ref,
    out_ref,
    fk_ref,
    fv_ref,
    fwq_ref,
    q_ref,
    kv_ref,
    fresh,
    outgo,
    total,
    core_in,
    *rest,
):
    seq = lax.axis_index("seq")
    side = lax.axis_index("head")
    count = lax.axis_size("seq")
    steps = len(levels)
    row_in = rest[:steps]
    row_out = rest[steps : 2 * steps]
    (
        attn,
        bias,
        fw_out,
        fw_in,
        core_sems,
        rs_sems,
        ag_sems,
        out_sems,
        fw_sems,
        halo_sems,
        fk_sems,
        fv_sems,
        w_sems,
        att_sems,
    ) = rest[2 * steps :]
    mats, hidden, width = total.shape
    rows = q_ref.shape[0]
    local_heads = fwq_ref.shape[1] // width
    half = local_heads // 2
    kv_heads = kv_ref.shape[2] // HD
    group = q_ref.shape[1] // HD // kv_heads
    core = lax.rem(seq, 2)
    mine, theirs = core * half, (1 - core) * half
    first = core * mats

    def partner(bit):
        return seq + bit * (1 - 2 * lax.rem(seq // bit, 2))

    def local(src, dst, sem):
        copy = pltpu.make_async_copy(src, dst, sem)
        copy.start()
        return copy

    order = []
    for lh in range(half):
        order += [theirs + lh, mine + lh]
    loads = []
    for slot, head in enumerate(order):
        cols = pl.ds(pl.multiple_of(head * width, width), width)
        loads.append(
            [
                local(fk_hbm.at[:, cols], fk_ref.at[slot], fk_sems.at[slot]),
                local(wg_hbm.at[head], fresh.at[head * 3], w_sems.at[0, slot]),
                local(wu_hbm.at[head], fresh.at[head * 3 + 1], w_sems.at[1, slot]),
                local(fv_hbm.at[:, cols], fv_ref.at[slot], fv_sems.at[slot]),
                local(wd_hbm.at[head], fresh.at[head * 3 + 2], w_sems.at[2, slot]),
            ]
        )
    att_loads = [
        local(q_hbm, q_ref, att_sems.at[0]),
        local(k_hbm, kv_ref.at[0, pl.ds(rows, rows)], att_sems.at[1]),
        local(v_hbm, kv_ref.at[1, pl.ds(rows, rows)], att_sems.at[2]),
    ]
    fwq_load = local(fwq_hbm, fwq_ref, att_sems.at[3])

    next_dev = (lax.rem(seq + side, count), 1 - side)
    prev_dev = (lax.rem(seq + count - 1 + side, count), 1 - side)
    barrier = pltpu.get_barrier_semaphore()
    for bit in (1,) + levels:
        pl.semaphore_signal(
            barrier, inc=1, device_id=(partner(bit), side), device_id_type=MESH
        )
    for target in ((seq, 1 - side), next_dev, prev_dev):
        pl.semaphore_signal(barrier, inc=1, device_id=target, device_id_type=MESH)
    pl.semaphore_wait(barrier, steps + 4)

    pending = []

    def send(src, dst, sems, where, target):
        copy = pltpu.make_async_remote_copy(
            src_ref=src,
            dst_ref=dst,
            send_sem=sems.at[(0,) + where],
            recv_sem=sems.at[(1,) + where],
            device_id=target,
            device_id_type=MESH,
        )
        copy.start()
        pending.append(copy)
        return copy

    halo = [
        send(src, kv_ref.at[i, pl.ds(0, rows)], halo_sems, (i,), next_dev)
        for i, src in enumerate((k_hbm, v_hbm))
    ]

    offsets = [0]
    for i, bit in enumerate(levels):
        offsets.append(offsets[-1] + lax.rem(seq // bit, 2) * (hidden >> (i + 1)))

    def held(i):
        size = hidden >> i
        return pl.ds(pl.multiple_of(offsets[i], size) if i else 0, size)

    def parts(i):
        size = hidden >> (i + 1)
        bit = lax.rem(seq // levels[i], 2)
        found = []
        for shift in (bit * size, (1 - bit) * size):
            found.append(
                (
                    pl.ds(pl.multiple_of(offsets[i] + shift, size), size),
                    pl.ds(pl.multiple_of(shift, size), size),
                )
            )
        return found

    core_copies = {}
    rs = {}
    ag = {}

    def split_send(i, m, arrived):
        kept, given = parts(i)
        row_out[i][m] = (total[m, given[0]] + arrived[m, given[1]].astype(F32)).astype(BF16)
        rs[i, m] = send(
            row_out[i].at[m], row_in[i].at[m], rs_sems, (i, m), (partner(levels[i]), side)
        )
        total[m, kept[0]] = total[m, kept[0]] + arrived[m, kept[1]].astype(F32)

    def core_sum(m):
        core_copies[m].wait_recv()
        split_send(0, m, core_in)

    def gather_send(i, m):
        where = fresh.at[first + m, held(i + 1)]
        ag[i, m] = send(where, where, ag_sems, (i, m), (partner(levels[i]), side))

    def row_sum(i, m):
        rs[i, m].wait_recv()
        if i + 1 < steps:
            split_send(i + 1, m, row_in[i])
        else:
            part = total[m, held(steps)] + row_in[i][m].astype(F32)
            old = fresh[first + m, held(steps)].astype(F32)
            new = old - part
            scale = jnp.sqrt(jnp.sum(old * old, axis=-1, keepdims=True)) / jnp.sqrt(
                jnp.sum(new * new, axis=-1, keepdims=True) + 1e-06
            )
            fresh[first + m, held(steps)] = (new * scale).astype(BF16)
            gather_send(steps - 1, m)

    def gathered(i, m):
        ag[i, m].wait_recv()
        if i > 0:
            gather_send(i - 1, m)
        else:
            where = fresh.at[first + m]
            ag[-1, m] = send(where, where, out_sems, (m,), (partner(1), side))

    def attend(kv):
        cols = slice(kv * HD, (kv + 1) * HD)
        keys = kv_ref[0, :, cols]
        values = kv_ref[1, :, cols]

        def one(j, carry):
            at = pl.ds(pl.multiple_of((kv * group + j) * HD, HD), HD)
            scores = mm(q_ref[:, at], keys, NT) * (HD**-0.5) + bias[...]
            expo = jnp.exp(scores - jnp.max(scores, axis=-1, keepdims=True))
            probs = (expo / jnp.sum(expo, axis=-1, keepdims=True)).astype(BF16)
            attn[:, at] = mm(probs, values, NN)
            return carry

        lax.fori_loop(0, group, one, 0)

    def apply_rows(head, start):
        cols = pl.ds(pl.multiple_of(head * width, width), width)
        query = fwq_ref[pl.ds(pl.multiple_of(start, rows), rows), cols]
        gate = mm(query, fresh[head * 3], NT)
        up = mm(query, fresh[head * 3 + 1], NT)
        mid = (gate * jax.nn.sigmoid(gate) * up).astype(BF16)
        raw = mm(mid, fresh[head * 3 + 2], NN)
        mean = jnp.mean(raw * raw, axis=-1, keepdims=True)
        return (raw * lax.rsqrt(mean + 1e-06) * gain_ref[:, cols]).astype(BF16)

    fw = {}

    def apply(slot, head):
        fw_out[slot] = apply_rows(head, (1 - side) * rows)
        fw[slot] = send(fw_out.at[slot], fw_in.at[slot], fw_sems, (slot,), (seq, 1 - side))
        local_part = apply_rows(head, side * rows)
        at = pl.ds(pl.multiple_of((side * local_heads + head) * width, width), width)
        out_ref[:, at] = (attn[:, at] + local_part.astype(F32)).astype(BF16)

    def finish(slot, head):
        fw[slot].wait_recv()
        at = pl.ds(pl.multiple_of(((1 - side) * local_heads + head) * width, width), width)
        out_ref[:, at] = (attn[:, at] + fw_in[slot].astype(F32)).astype(BF16)

    lane = lax.broadcasted_iota(jnp.int32, rate_ref.shape, 1)
    for slot, head in enumerate(order):
        for copy in loads[slot]:
            copy.wait()
        rate = jnp.sum(jnp.where(lane == head, rate_ref[...], 0.0), axis=1, keepdims=True)
        lh, own = slot // 2, slot % 2
        tiles = head_grads_tile(
            fk_ref[slot],
            fv_ref[slot],
            rate,
            fresh[head * 3],
            fresh[head * 3 + 1],
            fresh[head * 3 + 2],
        )
        made = []
        for kind, grad in tiles:
            m = 3 * lh + kind
            made.append(m)
            if own:
                total[m] = grad
            else:
                outgo[m] = grad.astype(BF16)
        for m in made:
            if own:
                core_sum(m)
            else:
                core_copies[m] = send(
                    outgo.at[m], core_in.at[m], core_sems, (m,), (partner(1), side)
                )

    base = (seq * 2 + side) * rows
    qpos = base + lax.broadcasted_iota(jnp.int32, bias.shape, 0)
    kpos = base - rows + lax.broadcasted_iota(jnp.int32, bias.shape, 1)
    valid = (kpos >= 0) & (kpos <= qpos) & (kpos > qpos - WINDOW)
    bias[...] = jnp.where(valid, 0.0, -1e30)
    for copy in att_loads:
        copy.wait()
    for copy in halo:
        copy.wait_recv()

    turn = [3 * lh + kind for lh in range(half) for kind in (2, 0, 1)]
    fillers = list(range(kv_heads))
    for wave in range(mats + 2 * steps - 1):
        for i in range(steps):
            if 0 <= wave - i < mats:
                row_sum(i, turn[wave - i])
        for j in range(steps - 1):
            if 0 <= wave - steps - j < mats:
                gathered(steps - 1 - j, turn[wave - steps - j])
        take = 2 if len(fillers) > mats - 1 - wave else 1
        for _ in range(take):
            if fillers:
                attend(fillers.pop(0))
    for kv in fillers:
        attend(kv)
    fwq_load.wait()
    for lh in range(half):
        for m in turn[3 * lh : 3 * lh + 3]:
            gathered(0, m)
        apply(lh, mine + lh)
        if lh > 0:
            for m in turn[3 * lh - 3 : 3 * lh]:
                ag[-1, m].wait_recv()
            apply(half + lh - 1, theirs + lh - 1)
    for m in turn[3 * half - 3 :]:
        ag[-1, m].wait_recv()
    apply(2 * half - 1, theirs + half - 1)
    for lh in range(half):
        finish(lh, mine + lh)
        if lh > 0:
            finish(half + lh - 1, theirs + lh - 1)
    finish(2 * half - 1, theirs + half - 1)
    for copy in pending:
        copy.wait_send()


def per_device(
    fw_keys,
    fw_values,
    fw_queries,
    rates,
    w_gate,
    w_up,
    w_down,
    out_gain,
    att_query,
    att_key,
    att_value,
):
    count = lax.axis_size("seq")
    local_heads, hidden, width = w_gate.shape
    rows = att_query.shape[0]
    fits = (
        lax.axis_size("head") == 2
        and count >= 4
        and count & (count - 1) == 0
        and local_heads % 2 == 0
        and hidden * 2 // count >= 16
        and rows == WINDOW
    )
    if not fits:
        return plain_device(
            fw_keys,
            fw_values,
            fw_queries,
            rates,
            w_gate,
            w_up,
            w_down,
            out_gain,
            att_query,
            att_key,
            att_value,
        )
    levels = []
    bit = 2
    while bit < count:
        levels.append(bit)
        bit *= 2
    levels = tuple(levels)
    steps = len(levels)
    tokens = fw_keys.shape[0]
    mats = 3 * local_heads // 2
    dma = pltpu.SemaphoreType.DMA
    vmem = pl.BlockSpec(memory_space=pltpu.VMEM)
    anywhere = pl.BlockSpec(memory_space=pl.ANY)
    lesser = [pltpu.VMEM((mats, hidden >> (i + 1), width), BF16) for i in range(steps)]
    return pl.pallas_call(
        functools.partial(block_kernel, levels),
        out_shape=jax.ShapeDtypeStruct(att_query.shape, BF16),
        in_specs=[anywhere] * 9 + [vmem] * 2,
        out_specs=vmem,
        scratch_shapes=[
            pltpu.VMEM((local_heads, tokens, width), BF16),
            pltpu.VMEM((local_heads, tokens, width), BF16),
            pltpu.VMEM(fw_queries.shape, BF16),
            pltpu.VMEM(att_query.shape, BF16),
            pltpu.VMEM((2, 2 * rows, att_key.shape[1]), BF16),
            pltpu.VMEM((2 * mats, hidden, width), BF16),
            pltpu.VMEM((mats, hidden, width), BF16),
            pltpu.VMEM((mats, hidden, width), F32),
            pltpu.VMEM((mats, hidden, width), BF16),
            *lesser,
            *lesser,
            pltpu.VMEM(att_query.shape, F32),
            pltpu.VMEM((rows, 2 * rows), F32),
            pltpu.VMEM((local_heads, rows, width), BF16),
            pltpu.VMEM((local_heads, rows, width), BF16),
            dma((2, mats)),
            dma((2, steps, mats)),
            dma((2, steps, mats)),
            dma((2, mats)),
            dma((2, local_heads)),
            dma((2, 2)),
            dma((local_heads,)),
            dma((local_heads,)),
            dma((3, local_heads)),
            dma((4,)),
        ],
        compiler_params=pltpu.CompilerParams(
            collective_id=0, has_side_effects=True, vmem_limit_bytes=60 * 2**20
        ),
    )(
        fw_keys,
        fw_values,
        fw_queries,
        w_gate,
        w_up,
        w_down,
        att_query,
        att_key,
        att_value,
        rates,
        out_gain.reshape(1, -1),
    )


def solution(mesh):
    return jax.shard_map(
        per_device,
        mesh=mesh,
        in_specs=(
            P("seq", "head"),
            P("seq", "head"),
            P("seq", "head"),
            P("seq", "head"),
            P("head", None, None),
            P("head", None, None),
            P("head", None, None),
            P("head"),
            P(("seq", "head"), None),
            P(("seq", "head"), None),
            P(("seq", "head"), None),
        ),
        out_specs=P(("seq", "head"), None),
        check_vma=False,
    )
```

```python
import functools

import jax
import jax.numpy as jnp
from jax import lax
from jax.experimental import pallas as pl
from jax.experimental.pallas import tpu as pltpu
from jax.sharding import PartitionSpec as P

HD = 128
WINDOW = 256
CUT = 2


def from_behind(block, axis, distance):
    devices = range(lax.axis_size(axis))
    route = [(i - distance, i) for i in devices if i - distance in devices]
    return lax.ppermute(block, axis, route)


def fast_hidden(inputs, w_gate, w_up):
    gate = jnp.dot(inputs, w_gate.T, preferred_element_type=jnp.float32)
    up = jnp.dot(inputs, w_up.T, preferred_element_type=jnp.float32)
    return (gate, up, (jax.nn.silu(gate) * up).astype(jnp.bfloat16))


def head_grads(keys, values, rate_col, w_gate, w_up, w_down):
    gate, up, hidden = fast_hidden(keys, w_gate, w_up)
    dval = (-rate_col[:, None] * values.astype(jnp.float32)).astype(jnp.bfloat16)
    g_down = jnp.dot(hidden.T, dval, preferred_element_type=jnp.float32)
    dhid = jnp.dot(dval, w_down.T, preferred_element_type=jnp.float32)
    sig = jax.nn.sigmoid(gate)
    d_gate = (dhid * up * sig * (1.0 + gate * (1.0 - sig))).astype(jnp.bfloat16)
    d_up = (dhid * (gate * sig)).astype(jnp.bfloat16)
    g_gate = jnp.dot(d_gate.T, keys, preferred_element_type=jnp.float32)
    g_up = jnp.dot(d_up.T, keys, preferred_element_type=jnp.float32)
    return jnp.stack([g_gate, g_up, g_down])


def renorm(old, grads):
    old = old.astype(jnp.float32)
    fresh = old - grads
    scale = jnp.sqrt(jnp.sum(old * old, axis=-1, keepdims=True)) / jnp.sqrt(
        jnp.sum(fresh * fresh, axis=-1, keepdims=True) + 1e-06
    )
    return (fresh * scale).astype(jnp.bfloat16)


def apply_head(queries, weights, gain):
    gate, up, hidden = fast_hidden(queries, weights[0], weights[1])
    raw = jnp.dot(hidden, weights[2], preferred_element_type=jnp.float32)
    normed = raw * lax.rsqrt(jnp.mean(raw * raw, axis=-1, keepdims=True) + 1e-06) * gain
    return normed.astype(jnp.bfloat16)


def plain_device(
    fw_keys,
    fw_values,
    fw_queries,
    rates,
    w_gate,
    w_up,
    w_down,
    out_gain,
    att_query,
    att_key,
    att_value,
):
    local_heads = w_gate.shape[0]
    width = w_gate.shape[2]
    stacked = jnp.stack([w_gate, w_up, w_down], axis=1)
    grad_list = []
    for head in range(local_heads):
        cols = slice(head * width, (head + 1) * width)
        grad_list.append(
            head_grads(
                fw_keys[:, cols],
                fw_values[:, cols],
                rates[:, head],
                w_gate[head],
                w_up[head],
                w_down[head],
            )
        )
    local_grads = jnp.stack(grad_list)
    shares = lax.psum_scatter(local_grads, "seq", scatter_dimension=2, tiled=True)
    count = shares.shape[2]
    first = lax.axis_index("seq") * count
    old_rows = lax.dynamic_slice_in_dim(stacked, first, count, 2)
    weights = lax.all_gather(renorm(old_rows, shares), "seq", axis=2, tiled=True)
    out_list = []
    for head in range(local_heads):
        cols = slice(head * width, (head + 1) * width)
        out_list.append(apply_head(fw_queries[:, cols], weights[head], out_gain[cols]))
    fw_local = jnp.concatenate(out_list, axis=1)
    fw_tok = lax.all_to_all(fw_local, "head", split_axis=0, concat_axis=1, tiled=True)
    rows = att_query.shape[0]
    kv_heads = att_key.shape[1] // HD
    group = att_query.shape[1] // HD // kv_heads
    reach = (WINDOW - 1) // rows + 1
    pair = jnp.stack([att_key, att_value])
    earlier = []
    moving = pair
    for step in range(reach):
        moving = from_behind(moving, ("seq", "head"), 1)
        earlier.insert(0, moving)
    window_kv = jnp.concatenate(earlier + [pair], axis=1)
    keys = window_kv[0].reshape(-1, kv_heads, HD)
    values = window_kv[1].reshape(-1, kv_heads, HD)
    base = (lax.axis_index("seq") * lax.axis_size("head") + lax.axis_index("head")) * rows
    qpos = base + jnp.arange(rows, dtype=jnp.int32)
    kpos = base - reach * rows + jnp.arange((reach + 1) * rows, dtype=jnp.int32)
    valid = (
        (kpos[None, :] >= 0)
        & (kpos[None, :] <= qpos[:, None])
        & (kpos[None, :] > qpos[:, None] - WINDOW)
    )
    query = att_query.reshape(rows, kv_heads, group, HD)
    scores = jnp.einsum(
        "rkgd,skd->kgrs", query, keys, preferred_element_type=jnp.float32
    ) / jnp.sqrt(jnp.float32(HD))
    scores = jnp.where(valid, scores, -1e30)
    peak = jnp.max(scores, axis=-1, keepdims=True)
    expo = jnp.exp(scores - peak)
    probs = (expo / jnp.sum(expo, axis=-1, keepdims=True)).astype(jnp.bfloat16)
    attn = jnp.einsum("kgrs,skd->rkgd", probs, values, preferred_element_type=jnp.float32).reshape(
        rows, -1
    )
    return (attn + fw_tok.astype(jnp.float32)).astype(jnp.bfloat16)


F32 = jnp.float32
BF16 = jnp.bfloat16
MESH = pl.DeviceIdType.MESH
NT = (((1,), (1,)), ((), ()))
TN = (((0,), (0,)), ((), ()))
NN = (((1,), (0,)), ((), ()))


def mm(a, b, dims):
    return lax.dot_general(a, b, dims, preferred_element_type=F32)


def head_grads_tile(keys, values, rate, w_gate, w_up, w_down):
    gate = mm(keys, w_gate, NT)
    up = mm(keys, w_up, NT)
    sig = jax.nn.sigmoid(gate)
    silu = gate * sig
    hidden = (silu * up).astype(BF16)
    dval = (-rate * values.astype(F32)).astype(BF16)
    dhid = mm(dval, w_down, NT)
    yield 2, mm(hidden, dval, TN)
    d_gate = (dhid * up * sig * (1.0 + gate * (1.0 - sig))).astype(BF16)
    yield 0, mm(d_gate, keys, TN)
    d_up = (dhid * silu).astype(BF16)
    yield 1, mm(d_up, keys, TN)


def block_kernel(
    levels,
    fk_hbm,
    fv_hbm,
    fwq_hbm,
    wg_hbm,
    wu_hbm,
    wd_hbm,
    q_hbm,
    k_hbm,
    v_hbm,
    rate_ref,
    gain_ref,
    out_ref,
    fk_ref,
    fv_ref,
    fwq_ref,
    q_ref,
    kv_ref,
    fresh,
    outgo,
    total,
    core_in,
    *rest,
):
    seq = lax.axis_index("seq")
    side = lax.axis_index("head")
    count = lax.axis_size("seq")
    steps = len(levels)
    row_in = rest[:steps]
    row_out = rest[steps : 2 * steps]
    (
        attn,
        bias,
        fw_out,
        fw_in,
        core_sems,
        rs_sems,
        ag_sems,
        out_sems,
        fw_sems,
        halo_sems,
        fk_sems,
        fv_sems,
        w_sems,
        att_sems,
    ) = rest[2 * steps :]
    mats, hidden, width = total.shape
    rows = q_ref.shape[0]
    local_heads = fwq_ref.shape[1] // width
    half = local_heads // 2
    kv_heads = kv_ref.shape[2] // HD
    group = q_ref.shape[1] // HD // kv_heads
    core = lax.rem(seq, 2)
    mine, theirs = core * half, (1 - core) * half
    first = core * mats

    def partner(bit):
        return seq + bit * (1 - 2 * lax.rem(seq // bit, 2))

    def local(src, dst, sem):
        copy = pltpu.make_async_copy(src, dst, sem)
        copy.start()
        return copy

    def matrix(head, kind):
        return pl.ds((head * 3 + kind) * CUT, CUT)

    def weight(head, kind):
        return fresh[matrix(head, kind)].reshape(CUT * hidden, width)

    order = []
    for lh in range(half):
        order += [theirs + lh, mine + lh]
    loads = []
    for slot, head in enumerate(order):
        cols = pl.ds(pl.multiple_of(head * width, width), width)
        loads.append(
            [
                local(fk_hbm.at[:, cols], fk_ref.at[slot], fk_sems.at[slot]),
                local(wg_hbm.at[head], fresh.at[matrix(head, 0)], w_sems.at[0, slot]),
                local(wu_hbm.at[head], fresh.at[matrix(head, 1)], w_sems.at[1, slot]),
                local(fv_hbm.at[:, cols], fv_ref.at[slot], fv_sems.at[slot]),
                local(wd_hbm.at[head], fresh.at[matrix(head, 2)], w_sems.at[2, slot]),
            ]
        )
    att_loads = [
        local(q_hbm, q_ref, att_sems.at[0]),
        local(k_hbm, kv_ref.at[0, pl.ds(rows, rows)], att_sems.at[1]),
        local(v_hbm, kv_ref.at[1, pl.ds(rows, rows)], att_sems.at[2]),
    ]
    fwq_load = local(fwq_hbm, fwq_ref, att_sems.at[3])

    next_dev = (lax.rem(seq + side, count), 1 - side)
    prev_dev = (lax.rem(seq + count - 1 + side, count), 1 - side)
    barrier = pltpu.get_barrier_semaphore()
    for bit in (1,) + levels:
        pl.semaphore_signal(
            barrier, inc=1, device_id=(partner(bit), side), device_id_type=MESH
        )
    for target in ((seq, 1 - side), next_dev, prev_dev):
        pl.semaphore_signal(barrier, inc=1, device_id=target, device_id_type=MESH)
    pl.semaphore_wait(barrier, steps + 4)

    pending = []

    def send(src, dst, sems, where, target):
        copy = pltpu.make_async_remote_copy(
            src_ref=src,
            dst_ref=dst,
            send_sem=sems.at[(0,) + where],
            recv_sem=sems.at[(1,) + where],
            device_id=target,
            device_id_type=MESH,
        )
        copy.start()
        pending.append(copy)
        return copy

    halo = [
        send(src, kv_ref.at[i, pl.ds(0, rows)], halo_sems, (i,), next_dev)
        for i, src in enumerate((k_hbm, v_hbm))
    ]

    offsets = [0]
    for i, bit in enumerate(levels):
        offsets.append(offsets[-1] + lax.rem(seq // bit, 2) * (hidden >> (i + 1)))

    def held(i):
        size = hidden >> i
        return pl.ds(pl.multiple_of(offsets[i], size) if i else 0, size)

    def parts(i):
        size = hidden >> (i + 1)
        bit = lax.rem(seq // levels[i], 2)
        found = []
        for shift in (bit * size, (1 - bit) * size):
            found.append(
                (
                    pl.ds(pl.multiple_of(offsets[i] + shift, size), size),
                    pl.ds(pl.multiple_of(shift, size), size),
                )
            )
        return found

    core_copies = {}
    rs = {}
    ag = {}

    def split_send(i, m, arrived):
        kept, given = parts(i)
        row_out[i][m] = (total[m, given[0]] + arrived[m, given[1]].astype(F32)).astype(BF16)
        rs[i, m] = send(
            row_out[i].at[m], row_in[i].at[m], rs_sems, (i, m), (partner(levels[i]), side)
        )
        total[m, kept[0]] = total[m, kept[0]] + arrived[m, kept[1]].astype(F32)

    def core_sum(m):
        core_copies[m].wait_recv()
        split_send(0, m, core_in)

    def gather_send(i, m):
        where = fresh.at[first + m, held(i + 1)]
        ag[i, m] = send(where, where, ag_sems, (i, m), (partner(levels[i]), side))

    def row_sum(i, m):
        rs[i, m].wait_recv()
        if i + 1 < steps:
            split_send(i + 1, m, row_in[i])
        else:
            part = total[m, held(steps)] + row_in[i][m].astype(F32)
            old = fresh[first + m, held(steps)].astype(F32)
            new = old - part
            scale = jnp.sqrt(jnp.sum(old * old, axis=-1, keepdims=True)) / jnp.sqrt(
                jnp.sum(new * new, axis=-1, keepdims=True) + 1e-06
            )
            fresh[first + m, held(steps)] = (new * scale).astype(BF16)
            gather_send(steps - 1, m)

    def gathered(i, m):
        ag[i, m].wait_recv()
        if i > 0:
            gather_send(i - 1, m)
        else:
            where = fresh.at[first + m]
            ag[-1, m] = send(where, where, out_sems, (m,), (partner(1), side))

    def attend(kv):
        cols = slice(kv * HD, (kv + 1) * HD)
        keys = kv_ref[0, :, cols]
        values = kv_ref[1, :, cols]

        def one(j, carry):
            at = pl.ds(pl.multiple_of((kv * group + j) * HD, HD), HD)
            scores = mm(q_ref[:, at], keys, NT) * (HD**-0.5) + bias[...]
            expo = jnp.exp(scores - jnp.max(scores, axis=-1, keepdims=True))
            probs = (expo / jnp.sum(expo, axis=-1, keepdims=True)).astype(BF16)
            attn[:, at] = mm(probs, values, NN)
            return carry

        lax.fori_loop(0, group, one, 0)

    def apply_rows(head, start):
        cols = pl.ds(pl.multiple_of(head * width, width), width)
        query = fwq_ref[pl.ds(pl.multiple_of(start, rows), rows), cols]
        gate = mm(query, weight(head, 0), NT)
        up = mm(query, weight(head, 1), NT)
        mid = (gate * jax.nn.sigmoid(gate) * up).astype(BF16)
        raw = mm(mid, weight(head, 2), NN)
        mean = jnp.mean(raw * raw, axis=-1, keepdims=True)
        return (raw * lax.rsqrt(mean + 1e-06) * gain_ref[:, cols]).astype(BF16)

    fw = {}

    def apply_send(slot, head):
        fw_out[slot] = apply_rows(head, (1 - side) * rows)
        fw[slot] = send(fw_out.at[slot], fw_in.at[slot], fw_sems, (slot,), (seq, 1 - side))

    def apply_own(head):
        local_part = apply_rows(head, side * rows)
        at = pl.ds(pl.multiple_of((side * local_heads + head) * width, width), width)
        out_ref[:, at] = (attn[:, at] + local_part.astype(F32)).astype(BF16)

    def finish(slot, head):
        fw[slot].wait_recv()
        at = pl.ds(pl.multiple_of(((1 - side) * local_heads + head) * width, width), width)
        out_ref[:, at] = (attn[:, at] + fw_in[slot].astype(F32)).astype(BF16)

    lane = lax.broadcasted_iota(jnp.int32, rate_ref.shape, 1)
    for slot, head in enumerate(order):
        for copy in loads[slot]:
            copy.wait()
        rate = jnp.sum(jnp.where(lane == head, rate_ref[...], 0.0), axis=1, keepdims=True)
        lh, own = slot // 2, slot % 2
        tiles = head_grads_tile(
            fk_ref[slot],
            fv_ref[slot],
            rate,
            weight(head, 0),
            weight(head, 1),
            weight(head, 2),
        )
        made = []
        for kind, grad in tiles:
            for cut in range(CUT):
                m = (3 * lh + kind) * CUT + cut
                made.append(m)
                piece = grad[cut * hidden : (cut + 1) * hidden]
                if own:
                    total[m] = piece
                else:
                    outgo[m] = piece.astype(BF16)
        for m in made:
            if own:
                core_sum(m)
            else:
                core_copies[m] = send(
                    outgo.at[m], core_in.at[m], core_sems, (m,), (partner(1), side)
                )

    base = (seq * 2 + side) * rows
    qpos = base + lax.broadcasted_iota(jnp.int32, bias.shape, 0)
    kpos = base - rows + lax.broadcasted_iota(jnp.int32, bias.shape, 1)
    valid = (kpos >= 0) & (kpos <= qpos) & (kpos > qpos - WINDOW)
    bias[...] = jnp.where(valid, 0.0, -1e30)
    for copy in att_loads:
        copy.wait()
    for copy in halo:
        copy.wait_recv()

    turn = [
        (3 * lh + kind) * CUT + cut
        for lh in range(half)
        for kind in (2, 0, 1)
        for cut in range(CUT)
    ]
    span = 3 * CUT
    fillers = list(range(kv_heads))
    for wave in range(mats + 2 * steps - 1):
        for i in range(steps):
            if 0 <= wave - i < mats:
                row_sum(i, turn[wave - i])
        for j in range(steps - 1):
            if 0 <= wave - steps - j < mats:
                gathered(steps - 1 - j, turn[wave - steps - j])
        take = 2 if len(fillers) > mats - 1 - wave else 1
        for _ in range(take):
            if fillers:
                attend(fillers.pop(0))
    for kv in fillers:
        attend(kv)
    fwq_load.wait()
    for lh in range(half):
        now = turn[span * lh : span * (lh + 1)]
        for m in now:
            gathered(0, m)
        apply_send(2 * lh, mine + lh)
        if lh + 1 < half:
            apply_own(mine + lh)
        for m in now:
            ag[-1, m].wait_recv()
        apply_send(2 * lh + 1, theirs + lh)
        if lh + 1 == half:
            apply_own(mine + lh)
        apply_own(theirs + lh)
    for lh in range(half):
        finish(2 * lh, mine + lh)
        finish(2 * lh + 1, theirs + lh)
    for copy in pending:
        copy.wait_send()


def per_device(
    fw_keys,
    fw_values,
    fw_queries,
    rates,
    w_gate,
    w_up,
    w_down,
    out_gain,
    att_query,
    att_key,
    att_value,
):
    count = lax.axis_size("seq")
    local_heads, hidden, width = w_gate.shape
    rows = att_query.shape[0]
    fits = (
        lax.axis_size("head") == 2
        and count >= 4
        and count & (count - 1) == 0
        and local_heads % 2 == 0
        and hidden * 2 // (count * CUT) >= 16
        and rows == WINDOW
    )
    if not fits:
        return plain_device(
            fw_keys,
            fw_values,
            fw_queries,
            rates,
            w_gate,
            w_up,
            w_down,
            out_gain,
            att_query,
            att_key,
            att_value,
        )
    levels = []
    bit = 2
    while bit < count:
        levels.append(bit)
        bit *= 2
    levels = tuple(levels)
    steps = len(levels)
    tokens = fw_keys.shape[0]
    mats = 3 * local_heads // 2 * CUT
    part = hidden // CUT
    pieces = (local_heads, CUT, part, width)
    dma = pltpu.SemaphoreType.DMA
    vmem = pl.BlockSpec(memory_space=pltpu.VMEM)
    anywhere = pl.BlockSpec(memory_space=pl.ANY)
    lesser = [pltpu.VMEM((mats, part >> (i + 1), width), BF16) for i in range(steps)]
    return pl.pallas_call(
        functools.partial(block_kernel, levels),
        out_shape=jax.ShapeDtypeStruct(att_query.shape, BF16),
        in_specs=[anywhere] * 9 + [vmem] * 2,
        out_specs=vmem,
        scratch_shapes=[
            pltpu.VMEM((local_heads, tokens, width), BF16),
            pltpu.VMEM((local_heads, tokens, width), BF16),
            pltpu.VMEM(fw_queries.shape, BF16),
            pltpu.VMEM(att_query.shape, BF16),
            pltpu.VMEM((2, 2 * rows, att_key.shape[1]), BF16),
            pltpu.VMEM((2 * mats, part, width), BF16),
            pltpu.VMEM((mats, part, width), BF16),
            pltpu.VMEM((mats, part, width), F32),
            pltpu.VMEM((mats, part, width), BF16),
            *lesser,
            *lesser,
            pltpu.VMEM(att_query.shape, F32),
            pltpu.VMEM((rows, 2 * rows), F32),
            pltpu.VMEM((local_heads, rows, width), BF16),
            pltpu.VMEM((local_heads, rows, width), BF16),
            dma((2, mats)),
            dma((2, steps, mats)),
            dma((2, steps, mats)),
            dma((2, mats)),
            dma((2, local_heads)),
            dma((2, 2)),
            dma((local_heads,)),
            dma((local_heads,)),
            dma((3, local_heads)),
            dma((4,)),
        ],
        compiler_params=pltpu.CompilerParams(
            collective_id=0, has_side_effects=True, vmem_limit_bytes=60 * 2**20
        ),
    )(
        fw_keys,
        fw_values,
        fw_queries,
        w_gate.reshape(pieces),
        w_up.reshape(pieces),
        w_down.reshape(pieces),
        att_query,
        att_key,
        att_value,
        rates,
        out_gain.reshape(1, -1),
    )


def solution(mesh):
    return jax.shard_map(
        per_device,
        mesh=mesh,
        in_specs=(
            P("seq", "head"),
            P("seq", "head"),
            P("seq", "head"),
            P("seq", "head"),
            P("head", None, None),
            P("head", None, None),
            P("head", None, None),
            P("head"),
            P(("seq", "head"), None),
            P(("seq", "head"), None),
            P(("seq", "head"), None),
        ),
        out_specs=P(("seq", "head"), None),
        check_vma=False,
    )
```
